512 devices in a mesh: req: 128 (over z, x, core), tp: 4 (over y).
Axes of the slice: x: 4, y: 4, z: 16, core: 2. Of those that a mesh axis runs over, the one named last changes fastest.
Arguments:
- tokens: bfloat16 [65536, 1408], P('req', 'tp'), may hold values from -24 to 24
- ln1_gain: float32 [1408], replicated, may hold values from 0.1 to 1.9
- ln1_bias: float32 [1408], replicated, may hold values from -3 to 3
- qkv_weight: bfloat16 [3, 1408, 1408], P(None, None, 'tp'), may hold values from -6 to 6
- out_weight: bfloat16 [1408, 1408], P('tp'), may hold values from -0.15625 to 0.15625
- ln2_gain: float32 [1408], replicated, may hold values from 0.25 to 1.75
- ln2_bias: float32 [1408], replicated, may hold values from -3 to 3
- merger_weight: bfloat16 [5632, 3584], P('req', 'tp'), may hold values from -0.078125 to 0.078125
- group_segments: int32 [128, 128], P('req'), may hold values from 0 to 7, never falling along the last dimension, each value on 1 to 41 neighbouring positions
- owners: int32 [16384, 1], P('req'), may hold values from 0 to 127; in each aligned block of 128 rows (0 to 127, 128 to 255, ...) at most 2 rows name the same one
Outputs:
- received: bfloat16 [32768, 3584], P('req', 'tp')
The draws below stay inside these ranges and needn't reach their ends.
Inputs may be any that keep to these rules, and one draw needn't show every extreme that they name: `group_segments`: never falling along a request's groups; every picture has 1 to 41 groups and one has exactly 41. `owners`: among the 128 groups of one request no owner appears more than 2 times; in every draw some request sends exactly 2 to some owner.
All inputs are finite; a program needn't handle non-finite values.
Results may differ from the reference program's by a relative error of at most 0.009.
Values may be sent and summed in bfloat16 or wider, within the bound.
No kernel may reach another device: no remote copies, remote signals or barrier semaphores. Data moves between devices by JAX's collectives and lax.ppermute only.
A program may use at most 128 MiB of HBM per device.

```python
import math
import jax
import jax.numpy as jnp
import numpy as np
from jax import lax

D = 1408
HEADS = 16
HEAD_DIM = 88
OUT = 3584
MERGE_DEV = 128
PICS = 8
TOK_DEV = 512
GMOST = 41
TOKENS = 65536
MERGED = 16384
CAP = 2
N_REQ = 128


def draw_tokens(key, part):
    key_base, key_cols, key_rows = jax.random.split(key, 3)
    ramp = 3.0 ** (jnp.arange(D, dtype=jnp.float32) / (D - 1))
    col_scale = ramp * jnp.exp(jax.random.uniform(key_cols, (D,), jnp.float32, math.log(0.3), math.log(3.0)))
    row_scale = jnp.exp(jax.random.uniform(key_rows, (TOKENS, 1), jnp.float32, math.log(0.3), math.log(3.0)))
    values = jax.random.normal(key_base, (TOKENS, D), jnp.float32) * row_scale * col_scale
    return jnp.clip(values, -24.0, 24.0).astype(jnp.bfloat16)


def draw_qkv_weight(key, part):
    key_base = jax.random.fold_in(key, 0)
    base = jax.random.normal(key_base, (3, D, D), jnp.float32) / math.sqrt(D)
    values = base
    return jnp.clip(values, -6.0, 6.0).astype(jnp.bfloat16)


def block_scale(own_key, shape, cuts, low, high):
    loudness, own = 1.0, jax.random.fold_in(own_key, 6)
    for axis_at, shards_of in cuts:
        heights = jnp.exp(jax.random.uniform(jax.random.fold_in(own, axis_at), (shards_of,), jnp.float32, low / len(cuts), high / len(cuts)))
        loudness = loudness * jnp.repeat(heights, shape[axis_at] // shards_of).reshape([-1 if axis == axis_at else 1 for axis in range(len(shape))])
    return loudness


def profile(amount, total, most, lean):
    loads = [(1 << 20) // math.isqrt(grade ** lean) + 1 for grade in range(2, amount + 1)]
    rest, counts = total - most - (amount - 1), [1] * (amount - 1)
    while rest > 0:
        candidates = [i for i in range(amount - 1) if counts[i] < most]
        mass, budget = sum([loads[i] for i in candidates]), rest
        for i in candidates:
            more = min(most - counts[i], max(1, budget * loads[i] // mass), rest)
            counts[i] = counts[i] + more
            rest = rest - more
    return np.array([most] + counts)


def uneven(rng, count, total, most, skew):
    if count == 2:
        one = jax.random.randint(rng, (), max(1, total - most), min(most, total - 1) + 1)
        return jnp.stack([one, total - one])
    sizes = jnp.asarray(profile(count, total, most, skew), jnp.int32)
    twos = (count - 1) // 2
    giver, receiver = sizes[1:1 + 2 * twos:2], sizes[2:2 + 2 * twos:2]
    slack = jnp.minimum(giver - 1, most - receiver)
    moved = jax.random.randint(jax.random.fold_in(rng, 1), (twos,), 0, 1 << 20) % (slack + 1)
    sizes = sizes.at[1:1 + 2 * twos:2].set(giver - moved).at[2:2 + 2 * twos:2].set(receiver + moved)
    return sizes[jax.random.permutation(jax.random.fold_in(rng, 2), count)]


def assign_block(stream_key, own, number, rows, amount, top, bound, slope):
    sequence = jax.random.permutation(stream_key, amount)
    packed, ordinary = shares(amount, rows * top, bound, slope, True), shares(amount, rows * top, bound, slope, False)
    places = jnp.arange(amount)

    def named(tallies, offset_by):
        used = int((tallies > 0).sum())
        fixed = max(1, used // 4)
        moved = fixed + (places - fixed + offset_by * (used - fixed)) % max(1, amount - fixed)
        return jnp.zeros((amount,), jnp.int32).at[sequence[jnp.where(places < fixed, places, moved)]].set(jnp.asarray(tallies, jnp.int32))

    tallies = jnp.where(number % 4 == 0, named(packed, number // 4), named(ordinary, number - number // 4 - 1))
    mixed = jax.random.permutation(jax.random.fold_in(own, 3), amount)
    donor, taker = mixed[0:amount // 2 * 2:2], mixed[1:amount // 2 * 2:2]
    room = jnp.minimum(tallies[donor] - 1, bound - tallies[taker]) // 2
    room = jnp.where((donor == sequence[0]) | (taker == sequence[0]) | (tallies[taker] == 0), 0, jnp.maximum(room, 0))
    moved = jax.random.randint(jax.random.fold_in(own, 4), (amount // 2,), 0, 1 << 20) % (room + 1)
    tallies = tallies.at[donor].add(-moved).at[taker].add(moved)
    members = jnp.searchsorted(jnp.cumsum(tallies), jnp.arange(rows * top), side="right").astype(jnp.int32)
    grid = members.reshape(top, rows).T
    grid = grid[jax.random.permutation(jax.random.fold_in(own, 1), rows)]
    offset_by = jax.random.randint(jax.random.fold_in(own, 2), (rows, 1), 0, top)
    return jnp.take_along_axis(grid, (jnp.arange(top)[None, :] + offset_by) % top, axis=1)


def shares(amount, total, bound, skew, full):
    loads = [(1 << 20) // math.isqrt(grade ** skew) + 1 for grade in range(1, amount + 1)]
    largest = bound if full else min(bound, max(-(-total // amount), total * loads[0] // sum(loads)))
    least = 1 if total - largest >= amount - 1 else 0
    counts, spare = [largest] + [least] * (amount - 1), total - largest - least * (amount - 1)
    while spare > 0:
        movable = [i for i in range(1, amount) if counts[i] < largest] or [i for i in range(1, amount) if counts[i] < bound]
        mass, remaining = sum([loads[i] for i in movable]), spare
        for i in movable:
            extra = min(bound - counts[i], max(1, remaining * loads[i] // mass), spare)
            counts[i] = counts[i] + extra
            spare = spare - extra
    return np.array(counts)


def bell_draw(own_key, shape, spread, reach, shards=(), kind=jnp.bfloat16):
    factor_of = block_scale(own_key, shape, shards, -0.22, 0.18) if shards else 1.0
    entries = jax.random.normal(own_key, shape, jnp.float32) * spread * factor_of
    return jnp.minimum(jnp.maximum(entries, -reach), reach).astype(kind)


def setup_inputs(seed: int = 0) -> dict:
    streams_of = jax.random.split(jax.random.key(seed), 11)
    tokens = draw_tokens(jax.random.fold_in(streams_of[10], 71), 0)
    ln1_gain = jnp.clip(1.0 + 0.18 * jax.random.normal(streams_of[1], (D,), jnp.float32), 0.1, 1.9)
    ln1_bias = bell_draw(streams_of[2], (D,), 0.5, 3.0, (), jnp.float32)
    qkv_weight = draw_qkv_weight(jax.random.fold_in(streams_of[10], 71), 0)
    out_weight = bell_draw(streams_of[4], (D, D), D ** -0.5, 0.15625, ((0, 4),))
    ln2_gain = jnp.clip(1.0 + 0.15 * jax.random.normal(streams_of[5], (D,), jnp.float32), 0.25, 1.75)
    ln2_bias = bell_draw(streams_of[6], (D,), 0.5, 3.0, (), jnp.float32)
    merger_weight = bell_draw(streams_of[7], (4 * D, OUT), (4 * D) ** -0.5, 0.078125, ((0, 128), (1, 4)))
    group_segments = jax.vmap(lambda own: jnp.searchsorted(jnp.cumsum(uneven(own, PICS, MERGE_DEV, GMOST, 2)), jnp.arange(MERGE_DEV), side="right"))(jax.random.split(streams_of[8], N_REQ)).reshape((N_REQ, MERGE_DEV)).astype(jnp.int32)
    owners_keys = jax.random.split(jax.random.fold_in(streams_of[9], 1), MERGED // MERGE_DEV)
    owners_turns = jax.random.permutation(jax.random.fold_in(streams_of[9], 3), MERGED // MERGE_DEV)
    owners = jax.vmap(lambda own, number: assign_block(jax.random.fold_in(streams_of[9], 2), own, number, MERGE_DEV, N_REQ, 1, CAP, 2))(owners_keys, owners_turns).reshape((MERGED, 1))
    return {"tokens": tokens, "ln1_gain": ln1_gain, "ln1_bias": ln1_bias, "qkv_weight": qkv_weight, "out_weight": out_weight, "ln2_gain": ln2_gain, "ln2_bias": ln2_bias, "merger_weight": merger_weight, "group_segments": group_segments, "owners": owners}


epsilon = 1e-06

def layer_norm(values, gain, bias):
    row_mean = lax.optimization_barrier(jnp.mean(values, axis=-1, keepdims=True))
    shifted = values - row_mean
    variance = lax.optimization_barrier(jnp.mean(shifted * shifted, axis=-1, keepdims=True))
    return shifted * lax.rsqrt(variance + epsilon) * gain + bias

def reference(tokens, ln1_gain, ln1_bias, qkv_weight, out_weight, ln2_gain, ln2_bias, merger_weight, group_segments, owners):
    qkv_float = qkv_weight.astype(jnp.float32)

    def encode(inputs):
        block, segment_row = inputs
        normed = layer_norm(block.astype(jnp.float32), ln1_gain, ln1_bias).astype(jnp.bfloat16)
        combined = jnp.einsum('td,cdh->cth', normed.astype(jnp.float32), qkv_float, precision=lax.Precision.HIGHEST)
        combined = combined.astype(jnp.bfloat16).astype(jnp.float32).reshape(3, TOK_DEV, HEADS, HEAD_DIM)
        scores = jnp.einsum('qhd,khd->hqk', combined[0], combined[1], precision=lax.Precision.HIGHEST) * HEAD_DIM ** (-0.5)
        segment_ids = jnp.repeat(segment_row, 4)
        same_picture = segment_ids[:, None] == segment_ids[None, :]
        scores = jnp.where(same_picture[None], scores, -1e+30)
        row_max = lax.optimization_barrier(jnp.max(scores, axis=2, keepdims=True))
        exponent = jnp.exp(scores - row_max)
        weights = (exponent / lax.optimization_barrier(jnp.sum(exponent, axis=2, keepdims=True))).astype(jnp.bfloat16)
        context = jnp.einsum('hqk,khd->qhd', weights.astype(jnp.float32), combined[2], precision=lax.Precision.HIGHEST)
        context = context.astype(jnp.bfloat16).reshape(TOK_DEV, D)
        hidden = block.astype(jnp.float32) + jnp.dot(context, out_weight, preferred_element_type=jnp.float32)
        patches = layer_norm(hidden, ln2_gain, ln2_bias).astype(jnp.bfloat16)
        flat = patches.reshape(MERGE_DEV, 4 * D)
        return jnp.dot(flat, merger_weight, preferred_element_type=jnp.float32).astype(jnp.bfloat16)
    projected = lax.map(encode, (tokens.reshape(N_REQ, TOK_DEV, D), group_segments))
    target = owners[:, 0].astype(jnp.int32).reshape(N_REQ, MERGE_DEV)
    owner_ids = jnp.arange(N_REQ).astype(jnp.int32)
    owner_hits = (target[:, :, None] == owner_ids[None, None, :]).astype(jnp.int32)
    before = (jnp.cumsum(owner_hits, axis=1).astype(jnp.int32) - owner_hits).astype(jnp.int32)
    slot_rank = lax.optimization_barrier(jnp.sum(before * owner_hits, axis=2)).astype(jnp.int32)
    destination = ((target * N_REQ + owner_ids[:, None]) * CAP + slot_rank).astype(jnp.int32).reshape(-1)
    received = jnp.zeros((N_REQ * N_REQ * CAP, OUT), jnp.bfloat16)
    return received.at[destination].set(projected.reshape(N_REQ * MERGE_DEV, OUT))
```

```python
import jax
import jax.numpy as jnp
from jax import lax
from jax.experimental import pallas as pl
from jax.experimental.pallas import tpu as pltpu
from jax.sharding import PartitionSpec as P


HEAD_DIM = 88
EPS = 1e-06
F32 = jnp.float32
BF16 = jnp.bfloat16
KIB = 1024
SMALL = 12 * 1024 * KIB
LARGE = 60 * 1024 * KIB
G1 = 51500 * KIB
G2 = 60 * 1024 * KIB
G3 = 49000 * KIB
VMEM = pl.BlockSpec(memory_space=pltpu.VMEM)
SMEM = pl.BlockSpec(memory_space=pltpu.SMEM)
HBM = pl.BlockSpec(memory_space=pltpu.HBM)
NZ, NX, NC = 16, 4, 2


def req_id(z, x, c):
    return (z * NX + x) * NC + c


def all_devices():
    return [(z, x, c) for z in range(NZ) for x in range(NX) for c in range(NC)]


def dot(a, b, ca=1, cb=0):
    return lax.dot_general(a, b, (((ca,), (cb,)), ((), ())), preferred_element_type=F32)


def call(body, out_shape, n_smem, n_vmem, grant):
    multi = isinstance(out_shape, (list, tuple))
    return pl.pallas_call(
        body,
        out_shape=out_shape,
        in_specs=[SMEM] * n_smem + [VMEM] * n_vmem,
        out_specs=[VMEM] * len(out_shape) if multi else VMEM,
        compiler_params=pltpu.CompilerParams(vmem_limit_bytes=grant),
    )


def regroup_kernel(x_ref, o_ref):
    n = x_ref.shape[1]
    src = lax.broadcasted_iota(jnp.int32, (n, n), 0)
    dst = lax.broadcasted_iota(jnp.int32, (n, n), 1)
    quarter = n // 4
    wanted = jnp.bitwise_and(dst * 4, n - 1) + lax.shift_right_logical(dst, quarter.bit_length() - 1)
    move = jnp.where(src == wanted, 1.0, 0.0).astype(BF16)
    moved = dot(x_ref[...], move).astype(BF16)
    for k in range(o_ref.shape[0]):
        o_ref[k] = moved


def assemble_kernel(x_at_ref, a_ref, b_ref, c_ref, d_ref, o_ref):
    rows = o_ref.shape[0]
    part = a_ref.shape[0]
    total = jnp.zeros(o_ref.shape, F32)
    for k, ref in enumerate((a_ref, b_ref, c_ref, d_ref)):
        base = lax.rem(x_at_ref[0] - k + NX, NX) * part
        row = lax.broadcasted_iota(jnp.int32, (rows, part), 0)
        col = lax.broadcasted_iota(jnp.int32, (rows, part), 1)
        place = jnp.where(row == col + base, 1.0, 0.0).astype(BF16)
        total = total + dot(place, ref[...])
    o_ref[...] = total.astype(BF16)


def attend_kernel(
    x_ref, gb_ref, w_hbm, wo_ref, seg_ref, part_hbm, norm, qkv, ctx, bias, w_ref, part_ref, w_sem, sem
):
    width, toks = x_ref.shape
    fetch = pltpu.make_async_copy(w_hbm, w_ref, w_sem)
    fetch.start()
    local_width = ctx.shape[0]
    heads = local_width // HEAD_DIM
    step = 176
    steps = width // step

    def rows(i):
        return pl.ds(pl.multiple_of(i * step, 8), step)

    def fold(v):
        return jnp.sum(v.reshape(step // 8, 8, toks), axis=0)

    def average(total):
        return jnp.sum(total, axis=0, keepdims=True) * (1.0 / width)

    start = jnp.zeros((8, toks), F32)
    mean = average(
        lax.fori_loop(0, steps, lambda i, acc: acc + fold(x_ref[rows(i), :].astype(F32)), start)
    )

    def spread(i, acc):
        d = x_ref[rows(i), :].astype(F32) - mean
        return acc + fold(d * d)

    var = average(lax.fori_loop(0, steps, spread, start))
    rstd = lax.rsqrt(var + EPS)

    def normalise(i, carry):
        d = x_ref[rows(i), :].astype(F32) - mean
        gb = gb_ref[rows(i), :]
        norm[rows(i), :] = (d * rstd * gb[:, 0:1] + gb[:, 1:2]).astype(BF16)
        return carry

    lax.fori_loop(0, steps, normalise, 0)

    fetch.wait()

    def project(i, carry):
        at = pl.ds(pl.multiple_of(i * local_width, 8), local_width)
        qkv[at, :] = dot(w_ref[at, :], norm[...])
        return carry

    lax.fori_loop(0, 3, project, 0)

    seg = jnp.concatenate([seg_ref[...]] * 4, axis=1).astype(F32)
    seg_rows = jnp.broadcast_to(seg, (8, toks))
    seg_cols = jnp.transpose(seg_rows)[:, 0:1]
    bias[...] = jnp.where(seg_cols == seg, 0.0, -1e30)

    for h in range(heads):
        q, k, v = (
            qkv[c * local_width + h * HEAD_DIM : c * local_width + (h + 1) * HEAD_DIM, :]
            for c in range(3)
        )
        s = dot(jnp.transpose(k).astype(BF16), q.astype(BF16)) * HEAD_DIM ** (-0.5) + bias[...]
        e = jnp.exp(s - jnp.max(s, axis=0, keepdims=True))
        total = jnp.sum(e, axis=0, keepdims=True)
        ctx[h * HEAD_DIM : (h + 1) * HEAD_DIM, :] = dot(v.astype(BF16), e.astype(BF16)) / total
    context = ctx[...].astype(BF16)
    quarter = toks // 4
    piece = 176

    def leave(i, p):
        at = pl.ds(pl.multiple_of(i * piece, 8), piece)
        return pltpu.make_async_copy(part_ref.at[p, at, :], part_hbm.at[p, at, :], sem.at[i, p])

    def outwards(i, carry):
        at = pl.ds(pl.multiple_of(i * piece, 8), piece)
        y = dot(wo_ref[at, :], context).astype(BF16)
        for p in range(4):
            part_ref[p, at, :] = y[:, p * quarter : (p + 1) * quarter]
            leave(i, p).start()
        return carry

    lax.fori_loop(0, width // piece, outwards, 0)

    def finish(i, carry):
        for p in range(4):
            leave(i, p).wait()
        return carry

    lax.fori_loop(0, width // piece, finish, 0)


def norm2_kernel(own_ref, part_ref, gb_ref, o_ref):
    hidden = own_ref[...].astype(F32)
    for p in range(4):
        hidden = hidden + part_ref[p].astype(F32)
    width = hidden.shape[0]
    mean = jnp.sum(hidden, axis=0, keepdims=True) * (1.0 / width)
    d = hidden - mean
    var = jnp.sum(d * d, axis=0, keepdims=True) * (1.0 / width)
    gb = jnp.transpose(gb_ref[...])
    out = (d * lax.rsqrt(var + EPS) * gb[:, 0:1] + gb[:, 1:2]).astype(BF16)
    half = width // 2
    for c in range(2):
        for p in range(4):
            o_ref[c * 4 + p] = out[c * half : (c + 1) * half, :]


def merge_kernel(core_ref, p_ref, w_hbm, mine_ref, other_ref, rhs, acc, sem):
    depth = rhs.shape[0]
    cuts = list(range(0, depth, 768)) + [depth]
    copies = []
    for n, (lo, hi) in enumerate(zip(cuts[:-1], cuts[1:])):
        at = pl.ds(lo, hi - lo)
        copies.append(pltpu.make_async_copy(w_hbm.at[at, :], rhs.at[at, :], sem.at[n]))
    for c in copies:
        c.start()
    lhs = jnp.concatenate(
        [jnp.concatenate([p_ref[p], p_ref[4 + p]], axis=1) for p in range(4)], axis=0
    )
    groups = mine_ref.shape[0]
    for n, (lo, hi) in enumerate(zip(cuts[:-1], cuts[1:])):
        copies[n].wait()
        y = dot(lhs[lo:hi, :], rhs[lo:hi, :], 0, 0)
        if n == 0:
            acc[...] = y
        else:
            acc[...] += y
    core = core_ref[0]
    mine_ref[...] = acc[pl.ds(pl.multiple_of(core * groups, groups), groups), :]
    other_ref[...] = acc[pl.ds(pl.multiple_of((1 - core) * groups, groups), groups), :]


def place_kernel(slot_ref, a_ref, b_ref, o_ref):
    projected = (a_ref[...] + b_ref[...]).astype(BF16)
    slots = o_ref.shape[0]
    row = lax.broadcasted_iota(jnp.int32, (slots, projected.shape[0]), 0)
    placing = jnp.where(row == slot_ref[...], 1.0, 0.0).astype(BF16)
    o_ref[...] = dot(placing, projected).astype(BF16)


def shape(dims, dtype=BF16):
    return jax.ShapeDtypeStruct(dims, dtype)


def feature_source(j, rows):
    z_rows = 8 * rows
    half = 2 * z_rows
    c, q = j // half, j % half
    z, x, row = q // (4 * rows), q % (4 * rows) // rows, q % rows
    return z * z_rows + (x * 2 + c) * rows + row


def layer(
    tokens,
    ln1_gain,
    ln1_bias,
    qkv_weight,
    out_weight,
    ln2_gain,
    ln2_bias,
    merger_weight,
    group_segments,
    owners,
):
    t = lax.axis_index("tp")
    r = lax.axis_index("req")
    core = lax.rem(r, NC)
    x_at = lax.rem(lax.div(r, NC), NX)
    toks, col_width = tokens.shape
    full_width = 4 * col_width
    groups = toks // 4
    out_cols = merger_weight.shape[1]
    rows_w = merger_weight.shape[0]
    capacity = 2

    rings = [[req_id(z, x, c) for z in range(NZ)] for x in range(NX) for c in range(NC)]
    pieces = [merger_weight]
    for k in range(1, NX):
        perm = [(req_id(z, x, c), req_id(z, (x + k) % NX, c)) for z, x, c in all_devices()]
        pieces.append(lax.ppermute(merger_weight, "req", perm))
    unit = call(assemble_kernel, shape((4 * rows_w, out_cols)), 1, 4, SMALL)(
        x_at.reshape(1).astype(jnp.int32), *pieces
    )
    weight = lax.all_gather(unit, "req", axis=0, axis_index_groups=rings, tiled=True)

    moved = call(regroup_kernel, shape((4, col_width, toks)), 0, 1, LARGE)(tokens.T)
    gathered = lax.all_to_all(moved, "tp", split_axis=0, concat_axis=0, tiled=True)
    gathered = gathered.reshape(full_width, toks)

    places = jnp.arange(full_width, dtype=jnp.int32)
    chosen = feature_source(places, rows_w)[:, None] == places[None, :]
    choose = chosen.astype(BF16)
    wo = dot(choose, out_weight, 1, 1).astype(BF16)

    parts = pl.pallas_call(
        attend_kernel,
        out_shape=shape((4, full_width, groups)),
        in_specs=[VMEM, VMEM, HBM, VMEM, VMEM],
        out_specs=HBM,
        scratch_shapes=[
            pltpu.VMEM((full_width, toks), BF16),
            pltpu.VMEM((3 * col_width, toks), F32),
            pltpu.VMEM((col_width, toks), F32),
            pltpu.VMEM((toks, toks), F32),
            pltpu.VMEM((3 * col_width, full_width), BF16),
            pltpu.VMEM((4, full_width, groups), BF16),
            pltpu.SemaphoreType.DMA,
            pltpu.SemaphoreType.DMA((full_width // 176, 4)),
        ],
        compiler_params=pltpu.CompilerParams(vmem_limit_bytes=G1),
    )(
        gathered,
        jnp.stack([ln1_gain, ln1_bias], axis=1),
        qkv_weight.swapaxes(1, 2).reshape(3 * col_width, full_width),
        wo,
        group_segments,
    )
    parts = lax.all_to_all(parts, "tp", split_axis=0, concat_axis=0, tiled=True)
    own = lax.dynamic_slice_in_dim(gathered, t * groups, groups, axis=1)
    own = dot(choose, own).astype(BF16)

    def reorder(v):
        return jnp.sum(jnp.where(chosen, v[None, :], 0.0), axis=1)[None, :]

    row = jnp.arange(8)[:, None]
    gain_bias = jnp.where(row == 0, reorder(ln2_gain), reorder(ln2_bias))
    patches = call(norm2_kernel, shape((8, full_width // 2, groups)), 0, 3, G2)(
        own, parts, gain_bias
    )
    members = [
        [req_id(z, x, c) * 4 + y for c in range(NC) for y in range(4)]
        for z in range(NZ)
        for x in range(NX)
    ]
    patches = lax.all_to_all(
        patches, ("req", "tp"), split_axis=0, concat_axis=0, tiled=True, axis_index_groups=members
    )

    half = full_width // 2
    swap = [(req_id(z, x, c), req_id(z, x, 1 - c)) for z, x, c in all_devices()]
    patches, weight = lax.optimization_barrier((patches, weight))
    part_mine, part_theirs = pl.pallas_call(
        merge_kernel,
        out_shape=[shape((groups, out_cols), F32)] * 2,
        in_specs=[SMEM, VMEM, HBM],
        out_specs=[VMEM] * 2,
        scratch_shapes=[
            pltpu.VMEM((4 * half, out_cols), BF16),
            pltpu.VMEM((2 * groups, out_cols), F32),
            pltpu.SemaphoreType.DMA((4,)),
        ],
        compiler_params=pltpu.CompilerParams(vmem_limit_bytes=G3),
    )(core.reshape(1).astype(jnp.int32), patches, weight)
    part_back = lax.ppermute(part_theirs, "req", swap)

    req_count = NZ * NX * NC
    slots = req_count * capacity
    target = owners[:, 0]
    earlier = jnp.arange(groups)[:, None] > jnp.arange(groups)[None, :]
    same = target[:, None] == target[None, :]
    rank = jnp.sum((earlier & same).astype(jnp.int32), axis=1)
    slot = (target * capacity + rank).reshape(1, groups)
    outgoing = call(place_kernel, shape((slots, out_cols)), 0, 3, SMALL)(slot, part_mine, part_back)
    outgoing = outgoing.reshape(req_count, capacity, out_cols)
    arrived = lax.all_to_all(outgoing, "req", split_axis=0, concat_axis=0, tiled=True)
    return arrived.reshape(slots, out_cols)


def solution(mesh):
    in_specs = (
        P("req", "tp"),
        P(),
        P(),
        P(None, None, "tp"),
        P("tp", None),
        P(),
        P(),
        P("req", "tp"),
        P("req", None),
        P("req", None),
    )
    out_specs = P("req", "tp")
    return jax.shard_map(layer, mesh=mesh, in_specs=in_specs, out_specs=out_specs, check_vma=False)
```
